32 devices in a mesh: group: 4 (over y, core), expert: 8 (over z, x).
Axes of the slice: x: 2, y: 2, z: 4, core: 2. Of those that a mesh axis runs over, the one named last changes fastest.
Arguments:
- tokens: bfloat16 [4096, 4096], P(('group', 'expert')), may hold values from -8 to 8
- router_weight: bfloat16 [4096, 128], replicated, may hold values from -4 to 4
- expert_dest: int32 [4096, 8], P(('group', 'expert')), may hold values from 0 to 127, all different within a row; in each aligned block of 128 rows (0 to 127, 128 to 255, ...) at most 9 rows name the same one
- group_capacity: int32 [4], replicated, may hold values from 4096 to 16383
- expert_capacity: int32 [128], replicated, may hold values from 128 to 511
- w_gate: bfloat16 [128, 4096, 768], P(('group', 'expert')), may hold values from -0.09375 to 0.09375
- w_up: bfloat16 [128, 4096, 768], P(('group', 'expert')), may hold values from -0.09375 to 0.09375
- w_down: bfloat16 [128, 768, 4096], P(('group', 'expert')), may hold values from -0.21875 to 0.21875
Outputs:
- mixed: bfloat16 [4096, 4096], P(('group', 'expert'))
- gating: float32 [4096, 8], P(('group', 'expert'))
The draws below stay inside these ranges and needn't reach their ends.
Inputs may be any that keep to these rules, and one draw needn't show every extreme that they name: `expert_dest`: each token names 8 different experts; among the tokens of one device no expert is named more than 9 times, and that bound is reached.
All inputs are finite; a program needn't handle non-finite values.
Results may differ from the reference program's by a relative error of at most 0.0058.
Values may be sent and summed in bfloat16 or wider, within the bound.
No kernel may reach another device: no remote copies, remote signals or barrier semaphores. Data moves between devices by JAX's collectives and lax.ppermute only.
A program may use at most 256 MiB of HBM per device.

```python
import math
import jax
import jax.numpy as jnp
import numpy as np
from jax import lax

D = 4096
FF = 768
EXPERTS = 128
TOPK = 8
ITER1 = 10
ITER2 = 10
TOK_DEV = 128
TOKENS = 4096
GROUP_EXPERTS = 32
SLOT_CAP = 9
N_GROUP = 4
N_EXPERT = 8


def drawn_amplitude():
    return 3.0 / max(1, D // EXPERTS)


def draw_tokens(key, part):
    blocks = TOKENS // TOK_DEV
    n_groups = EXPERTS // GROUP_EXPERTS
    block_index = jnp.arange(blocks, dtype=jnp.int32)
    shift = jax.random.randint(jax.random.fold_in(key, 106), (), 0, n_groups)
    chosen_group = (block_index * n_groups // blocks + shift) % n_groups
    first_offset = jax.random.randint(jax.random.fold_in(key, 102), (blocks,), 0, GROUP_EXPERTS)
    stride = jax.random.randint(jax.random.fold_in(key, 103), (blocks,), 1, GROUP_EXPERTS // 4 + 1)
    members = jnp.arange(4, dtype=jnp.int32)
    chosen = chosen_group[:, None] * GROUP_EXPERTS + (first_offset[:, None] + members[None, :] * stride[:, None]) % GROUP_EXPERTS
    feature = jnp.arange(D, dtype=jnp.int32)
    hits = feature[None, :, None] % EXPERTS == chosen[:, None, :] % D
    member_mask = jnp.any(hits, 2).astype(jnp.float32)
    noise = jnp.clip(jax.random.normal(jax.random.fold_in(key, 104), (blocks, TOK_DEV, D), jnp.float32), -5.0, 5.0)
    strength = jax.random.uniform(jax.random.fold_in(key, 105), (blocks, TOK_DEV, 1), jnp.float32, 0.7, 1.3)
    values = noise + 1.5 * strength * member_mask[:, None, :]
    return values.reshape(TOKENS, D).astype(jnp.bfloat16)


def draw_router_weight(key, part):
    feature = jnp.arange(D, dtype=jnp.int32)[:, None]
    column = jnp.arange(EXPERTS, dtype=jnp.int32)[None, :]
    planted = (feature % EXPERTS == column % D).astype(jnp.float32)
    base = jnp.clip(jax.random.normal(jax.random.fold_in(key, 201), (D, EXPERTS), jnp.float32), -5.0, 5.0)
    lift = jax.random.uniform(jax.random.fold_in(key, 202), (D, EXPERTS), jnp.float32, 0.8, 1.2)
    values = base * D ** (-0.5) + drawn_amplitude() * lift * planted
    return values.astype(jnp.bfloat16)


def plant(values, rng, low, largest):
    place = [jax.random.randint(jax.random.fold_in(rng, axis), (), 0, length) for axis, length in enumerate(values.shape)]
    main_axis = values.shape.index(max(values.shape))
    beside = place[:main_axis] + [(place[main_axis] + 1) % values.shape[main_axis]] + place[main_axis + 1:]
    return values.at[tuple(place)].set(low).at[tuple(beside)].set(largest)


def levels(key, shape, pieces, least, high):
    def one(dim, blocks):
        steps = jax.random.uniform(jax.random.fold_in(jax.random.fold_in(key, 6), dim), (blocks,), jnp.float32, least / len(pieces), high / len(pieces))
        return jnp.repeat(jnp.exp(steps), shape[dim] // blocks).reshape((-1,) + (1,) * (len(shape) - dim - 1))

    factor_of = one(*pieces[0])
    for cut in pieces[1:]:
        factor_of = factor_of * one(*cut)
    return factor_of


def assign_block(rng, own, number, rows, number_of, top, most, lean):
    sequence = jax.random.permutation(rng, number_of)
    crowded, ordinary = shares(number_of, rows * top, most, lean, True), shares(number_of, rows * top, most, lean, False)
    places = jnp.arange(number_of)

    def named(lengths, turn):
        used = int((lengths > 0).sum())
        fixed = max(1, used // 4)
        shifted = fixed + (places - fixed + turn * (used - fixed)) % max(1, number_of - fixed)
        return jnp.zeros((number_of,), jnp.int32).at[sequence[jnp.where(places < fixed, places, shifted)]].set(jnp.asarray(lengths, jnp.int32))

    lengths = jnp.where(number % 4 == 0, named(crowded, number // 4), named(ordinary, number - number // 4 - 1))
    mixed = jax.random.permutation(jax.random.fold_in(own, 3), number_of)
    giver, taker = mixed[0:number_of // 2 * 2:2], mixed[1:number_of // 2 * 2:2]
    room = jnp.minimum(lengths[giver] - 1, most - lengths[taker]) // 2
    room = jnp.where((giver == sequence[0]) | (taker == sequence[0]) | (lengths[taker] == 0), 0, jnp.maximum(room, 0))
    shifted = jax.random.randint(jax.random.fold_in(own, 4), (number_of // 2,), 0, 1 << 20) % (room + 1)
    lengths = lengths.at[giver].add(-shifted).at[taker].add(shifted)
    items = jnp.searchsorted(jnp.cumsum(lengths), jnp.arange(rows * top), side="right").astype(jnp.int32)
    table = items.reshape(top, rows).T
    table = table[jax.random.permutation(jax.random.fold_in(own, 1), rows)]
    turn = jax.random.randint(jax.random.fold_in(own, 2), (rows, 1), 0, top)
    return jnp.take_along_axis(table, (jnp.arange(top)[None, :] + turn) % top, axis=1)


def shares(number_of, total, limit, lean, full):
    loads = [(1 << 20) // math.isqrt(grade ** lean) + 1 for grade in range(1, number_of + 1)]
    largest = limit if full else min(limit, max(-(-total // number_of), total * loads[0] // sum(loads)))
    least = 1 if total - largest >= number_of - 1 else 0
    holding, surplus = [largest] + [least] * (number_of - 1), total - largest - least * (number_of - 1)
    while surplus > 0:
        free = [i for i in range(1, number_of) if holding[i] < largest] or [i for i in range(1, number_of) if holding[i] < limit]
        pool, left = sum([loads[i] for i in free]), surplus
        for i in free:
            addition = min(limit - holding[i], max(1, left * loads[i] // pool), surplus)
            holding[i] = holding[i] + addition
            surplus = surplus - addition
    return np.array(holding)


def scatter_about(own_key, dims, spread, most, shards=(), held_as=jnp.bfloat16):
    entries = spread * jax.random.normal(own_key, dims, jnp.float32)
    if shards:
        entries = entries * levels(own_key, dims, shards, -0.22, 0.18)
    return jnp.clip(entries, -most, most).astype(held_as)


def setup_inputs(seed: int = 0) -> dict:
    splits = jax.random.split(jax.random.key(seed), 9)
    tokens = draw_tokens(jax.random.fold_in(splits[8], 71), 0)
    router_weight = draw_router_weight(jax.random.fold_in(splits[8], 71), 0)
    expert_dest_keys = jax.random.split(jax.random.fold_in(splits[2], 1), TOKENS // TOK_DEV)
    expert_dest_turns = jax.random.permutation(jax.random.fold_in(splits[2], 3), TOKENS // TOK_DEV)
    expert_dest = jax.vmap(lambda own, number: assign_block(jax.random.fold_in(splits[2], 2), own, number, TOK_DEV, EXPERTS, TOPK, SLOT_CAP, 0))(expert_dest_keys, expert_dest_turns).reshape((TOKENS, TOPK))
    group_capacity = plant(jax.random.randint(splits[3], (N_GROUP,), TOK_DEV * N_EXPERT * TOPK // 2, TOK_DEV * N_EXPERT * TOPK * 2), jax.random.fold_in(splits[3], 1), TOK_DEV * N_EXPERT * TOPK // 2, (TOK_DEV * N_EXPERT * TOPK * 2) - 1).astype(jnp.int32)
    expert_capacity = plant(jax.random.randint(splits[4], (EXPERTS,), TOKENS * TOPK // (2 * EXPERTS), TOKENS * TOPK * 2 // EXPERTS), jax.random.fold_in(splits[4], 1), TOKENS * TOPK // (2 * EXPERTS), (TOKENS * TOPK * 2 // EXPERTS) - 1).astype(jnp.int32)
    w_gate = scatter_about(splits[5], (EXPERTS, D, FF), D ** -0.5, 0.09375, ((0, 32),))
    w_up = scatter_about(splits[6], (EXPERTS, D, FF), D ** -0.5, 0.09375, ((0, 32),))
    w_down = scatter_about(splits[7], (EXPERTS, FF, D), FF ** -0.5, 0.21875, ((0, 32),))
    return {"tokens": tokens, "router_weight": router_weight, "expert_dest": expert_dest, "group_capacity": group_capacity, "expert_capacity": expert_capacity, "w_gate": w_gate, "w_up": w_up, "w_down": w_down}


def balance(scores, gtarget, etarget):
    rows = scores.shape[0]
    blocks = scores.reshape(rows, N_GROUP, EXPERTS // N_GROUP)
    kernel = jnp.sum(blocks, 2)

    def first(step, carry):
        scale_rows, scale_cols = carry
        scale_rows = 1.0 / jnp.sum(kernel * scale_cols[None, :], 1)
        scale_cols = gtarget / jnp.sum(kernel * scale_rows[:, None], 0)
        return scale_rows, scale_cols

    scale_rows, scale_cols = lax.fori_loop(0, ITER1, first, (jnp.ones((rows,), jnp.float32), jnp.ones((N_GROUP,), jnp.float32)))
    plan = scale_rows[:, None] * kernel * scale_cols[None, :]

    def second(step, carry):
        row_fac, col_fac = carry
        row_fac = plan / jnp.sum(blocks * col_fac[None], 2)
        col_fac = etarget / jnp.sum(blocks * row_fac[:, :, None], 0)
        return row_fac, col_fac

    row_fac, col_fac = lax.fori_loop(0, ITER2, second, (jnp.ones((rows, N_GROUP), jnp.float32), jnp.ones((N_GROUP, EXPERTS // N_GROUP), jnp.float32)))
    return (row_fac[:, :, None] * blocks * col_fac[None]).reshape(rows, EXPERTS)


def reference(tokens, router_weight, expert_dest, group_capacity, expert_capacity, w_gate, w_up, w_down):
    logits = jnp.dot(tokens, router_weight, preferred_element_type=jnp.float32)
    scores = jnp.exp(logits)
    gcap = group_capacity.astype(jnp.float32)
    gtarget = TOKENS * gcap / jnp.sum(gcap)
    ecap = expert_capacity.astype(jnp.float32).reshape(N_GROUP, EXPERTS // N_GROUP)
    etarget = (gtarget / jnp.sum(ecap, 1))[:, None] * ecap
    balanced = balance(scores, gtarget, etarget)
    gating = jnp.take_along_axis(balanced, expert_dest, axis=1) * (EXPERTS / TOPK)
    devices = N_GROUP * N_EXPERT
    flat = expert_dest.reshape(devices, TOK_DEV * TOPK)
    onehot = (flat[:, :, None] == jnp.arange(EXPERTS, dtype=jnp.int32)[None, None, :]).astype(jnp.int32)
    rank = jnp.sum(jnp.cumsum(onehot, 1) * onehot, 2) - 1
    source = jnp.arange(devices, dtype=jnp.int32)[:, None]
    per_expert_rows = devices * SLOT_CAP
    slot = (flat * per_expert_rows + source * SLOT_CAP + rank).reshape(-1).astype(jnp.int32)
    token_id = (jnp.arange(TOKENS * TOPK, dtype=jnp.int32) // TOPK).astype(jnp.int32)
    table = jnp.zeros((EXPERTS * per_expert_rows,), jnp.int32).at[slot].set(token_id).reshape(EXPERTS, per_expert_rows)
    weights = jnp.zeros((EXPERTS * per_expert_rows,), jnp.float32).at[slot].set(gating.reshape(-1)).reshape(EXPERTS, per_expert_rows)

    def per_expert(total, item):
        index, wts, gate_w, up_w, down_w = item
        rows = tokens[index]
        gate = jnp.dot(rows, gate_w, preferred_element_type=jnp.float32)
        up = jnp.dot(rows, up_w, preferred_element_type=jnp.float32)
        hidden = (jax.nn.silu(gate) * up).astype(jnp.bfloat16)
        output = jnp.dot(hidden, down_w, preferred_element_type=jnp.float32).astype(jnp.bfloat16)
        return total.at[index].add(wts[:, None] * output.astype(jnp.float32)), None

    total, _ = lax.scan(per_expert, jnp.zeros((TOKENS, D), jnp.float32), (table, weights, w_gate, w_up, w_down))
    return total.astype(jnp.bfloat16), gating
```

```python
import functools

import jax
import jax.numpy as jnp
from jax import lax
from jax.experimental import pallas as pl
from jax.experimental.pallas import tpu as pltpu
from jax.sharding import Mesh
from jax.sharding import PartitionSpec as P

ITER1 = 10
ITER2 = 10
SLOT_CAP = 9
MAIN = 8

ALL = ("group", "plane", "side")
PLANE = ("group", "side")
VMEM = pl.BlockSpec(memory_space=pltpu.VMEM)
SMEM = pl.BlockSpec(memory_space=pltpu.SMEM)
BIG = pltpu.CompilerParams(vmem_limit_bytes=60 << 20)


def round_up(value, step):
    return -(-value // step) * step


def piece_rows(exp_dev):
    return round_up(2 * exp_dev * SLOT_CAP, 8)


def row_slots(exp_dev, shape):
    row = lax.broadcasted_iota(jnp.int32, shape, 0)
    last = row - 2 * MAIN * exp_dev
    main = last < 0
    expert = jnp.where(main, lax.shift_right_logical(row, 4), lax.shift_right_logical(last, 1))
    half = jnp.where(main, lax.shift_right_logical(row, 3) & 1, last & 1)
    rank = jnp.where(main, row & 7, MAIN)
    slot = jnp.where(last >= 2 * exp_dev, -1, expert * SLOT_CAP + rank)
    return slot, half


def pack_kernel(exp_dev, dst_ref, slot_ref, tok_ref, *outs):
    rows, half_width = outs[0].shape
    topk, count = slot_ref.shape
    local, half = row_slots(exp_dev, (rows, count))
    low, high = [], []
    for k in range(len(outs)):
        want = jnp.where(local < 0, -1, local + dst_ref[k] * (exp_dev * SLOT_CAP))
        hit = jnp.zeros((rows, count), jnp.float32)
        for i in range(topk):
            hit = jnp.where(slot_ref[i : i + 1, :] == want, 1.0, hit)
        low.append(jnp.where(half == 0, hit, 0.0))
        high.append(jnp.where(half == 1, hit, 0.0))
    low = jnp.concatenate(low, 0).astype(jnp.bfloat16)
    high = jnp.concatenate(high, 0).astype(jnp.bfloat16)
    step = min(512, half_width)
    for c in range(0, half_width, step):
        got = jnp.dot(low, tok_ref[:, c : c + step], preferred_element_type=jnp.float32)
        got += jnp.dot(
            high,
            tok_ref[:, half_width + c : half_width + c + step],
            preferred_element_type=jnp.float32,
        )
        for k, out in enumerate(outs):
            out[:, c : c + step] = got[k * rows : (k + 1) * rows].astype(jnp.bfloat16)


def pack(exp_dev, dst, slot, tok):
    rows, width = piece_rows(exp_dev), tok.shape[1]
    n = dst.shape[0]
    return pl.pallas_call(
        functools.partial(pack_kernel, exp_dev),
        out_shape=[jax.ShapeDtypeStruct((rows, width // 2), jnp.bfloat16)] * n,
        in_specs=[SMEM, VMEM, VMEM],
        out_specs=[VMEM] * n,
        compiler_params=BIG,
        cost_estimate=pl.CostEstimate(
            flops=2 * n * rows * tok.shape[0] * width,
            bytes_accessed=2 * tok.size + n * rows * width,
            transcendentals=0,
        ),
        name="pack",
    )(dst, slot, tok)


def ffn_kernel(n, exp_dev, *refs):
    pieces, (wg_ref, wu_ref, wd_ref) = refs[:n], refs[n : n + 3]
    outs = refs[n + 3 : 2 * n + 3]
    x_ref, acc_ref, last_ref, res_ref = refs[2 * n + 3 :]
    e, f = pl.program_id(0), pl.program_id(1)
    half_width = pieces[0].shape[1]
    first = 2 * MAIN * exp_dev
    step = min(1024, half_width)

    @pl.when((e == 0) & (f == 0))
    def _():
        for c in range(0, half_width, step):
            tiles = [p[first : first + 8, c : c + step].astype(jnp.float32) for p in pieces]
            last_ref[:, c : c + step] = jnp.concatenate(tiles, 0).astype(jnp.bfloat16)

    @pl.when(f == 0)
    def _():
        at = pl.multiple_of(e * 2 * MAIN, 2 * MAIN)
        for i in range(0, n, 2):
            for c in range(0, half_width, step):
                a = pieces[i][pl.ds(at, 2 * MAIN), c : c + step].astype(jnp.float32)
                b = pieces[i + 1][pl.ds(at, 2 * MAIN), c : c + step].astype(jnp.float32)
                for h in range(2):
                    both = jnp.concatenate([a[h * 8 : h * 8 + 8], b[h * 8 : h * 8 + 8]], 0)
                    x_ref[i * 8 : i * 8 + 16, h * half_width + c : h * half_width + c + step] = (
                        both.astype(jnp.bfloat16)
                    )
        row = lax.broadcasted_iota(jnp.int32, (n, 8 * n), 0)
        col = lax.broadcasted_iota(jnp.int32, (n, 8 * n), 1)
        for h in range(2):
            pick = jnp.where(col == row * 8 + e * 2 + h, 1.0, 0.0).astype(jnp.bfloat16)
            for c in range(0, half_width, step):
                x_ref[8 * n :, h * half_width + c : h * half_width + c + step] = jnp.dot(
                    pick, last_ref[:, c : c + step], preferred_element_type=jnp.float32
                ).astype(jnp.bfloat16)
        acc_ref[...] = jnp.zeros_like(acc_ref)

    x = x_ref[...]
    gate = jnp.dot(x, wg_ref[0], preferred_element_type=jnp.float32)
    up = jnp.dot(x, wu_ref[0], preferred_element_type=jnp.float32)
    hidden = (gate / (1.0 + jnp.exp(-gate)) * up).astype(jnp.bfloat16)
    for c in range(0, 2 * half_width, step):
        acc_ref[:, c : c + step] += jnp.dot(
            hidden, wd_ref[0, :, c : c + step], preferred_element_type=jnp.float32
        )

    @pl.when(f == pl.num_programs(1) - 1)
    def _():
        at = pl.multiple_of(e * 2 * MAIN, 2 * MAIN)
        for i in range(n):
            for c in range(0, half_width, step):
                both = jnp.concatenate(
                    [
                        acc_ref[i * 8 : i * 8 + 8, h * half_width + c : h * half_width + c + step]
                        for h in range(2)
                    ],
                    0,
                )
                outs[i][pl.ds(at, 2 * MAIN), c : c + step] = both.astype(jnp.bfloat16)
        res_ref[pl.ds(pl.multiple_of(e * n, n), n), :] = acc_ref[8 * n :, :].astype(jnp.bfloat16)

    @pl.when((f == pl.num_programs(1) - 1) & (e == exp_dev - 1))
    def _():
        row = lax.broadcasted_iota(jnp.int32, (8 * n, exp_dev * n), 0)
        col = lax.broadcasted_iota(jnp.int32, (8 * n, exp_dev * n), 1)
        place = lax.shift_right_logical(row, 3)
        expert = lax.shift_right_logical(row & 7, 1)
        hit = col == expert * n + place
        for c in range(0, half_width, step):
            got = None
            for h in range(2):
                pick = jnp.where(hit & ((row & 1) == h), 1.0, 0.0).astype(jnp.bfloat16)
                term = jnp.dot(
                    pick,
                    res_ref[:, h * half_width + c : h * half_width + c + step],
                    preferred_element_type=jnp.float32,
                )
                got = term if got is None else got + term
            for i in range(n):
                outs[i][first : first + 8, c : c + step] = got[i * 8 : i * 8 + 8].astype(
                    jnp.bfloat16
                )


def ffn(pieces, w_gate, w_up, w_down):
    n = len(pieces)
    exp_dev, width, hidden = w_gate.shape
    rows, half_width = pieces[0].shape
    tile = 256 if hidden % 256 == 0 else hidden
    whole = pl.BlockSpec((rows, half_width), lambda e, f: (0, 0), pipeline_mode=pl.Buffered(1))
    made = pl.BlockSpec((rows, half_width), lambda e, f: (0, 0), pipeline_mode=pl.Buffered(1))
    total = SLOT_CAP * n
    return pl.pallas_call(
        functools.partial(ffn_kernel, n, exp_dev),
        grid=(exp_dev, hidden // tile),
        out_shape=[jax.ShapeDtypeStruct((rows, half_width), jnp.bfloat16)] * n,
        in_specs=[whole] * n
        + [pl.BlockSpec((1, width, tile), lambda e, f: (e, 0, f))] * 2
        + [pl.BlockSpec((1, tile, width), lambda e, f: (e, f, 0))],
        out_specs=[made] * n,
        scratch_shapes=[
            pltpu.VMEM((total, width), jnp.bfloat16),
            pltpu.VMEM((total, width), jnp.float32),
            pltpu.VMEM((8 * n, half_width), jnp.bfloat16),
            pltpu.VMEM((exp_dev * n, width), jnp.bfloat16),
        ],
        compiler_params=pltpu.CompilerParams(
            dimension_semantics=("arbitrary", "arbitrary"), vmem_limit_bytes=60 << 20
        ),
        cost_estimate=pl.CostEstimate(
            flops=6 * exp_dev * total * width * hidden,
            bytes_accessed=6 * exp_dev * width * hidden + 4 * n * rows * half_width,
            transcendentals=exp_dev * total * hidden,
        ),
        name="ffn",
    )(*pieces, w_gate, w_up, w_down)


def combine_kernel(exp_dev, n, dst_ref, slot_ref, gate_ref, *refs):
    pieces, others, out_ref = refs[:n], refs[n:-1], refs[-1]
    rows, half_width = pieces[0].shape
    topk, count = slot_ref.shape
    local, half = row_slots(exp_dev, (rows, count))
    weights = []
    for k in range(n):
        want = jnp.where(local < 0, -1, local + dst_ref[k] * (exp_dev * SLOT_CAP))
        weight = jnp.zeros((rows, count), jnp.float32)
        for i in range(topk):
            weight = jnp.where(slot_ref[i : i + 1, :] == want, gate_ref[i : i + 1, :], weight)
        coarse = weight.astype(jnp.bfloat16).astype(jnp.float32)
        rest = weight - coarse
        weights.append(
            jnp.concatenate(
                [jnp.where(half == h, part, 0.0) for part in (coarse, rest) for h in range(2)], 1
            ).astype(jnp.bfloat16)
        )
    step = min(512, half_width)
    for c in range(0, half_width, step):
        total = None
        for weight, piece in zip(weights, pieces):
            term = lax.dot_general(
                weight,
                piece[:, c : c + step],
                (((0,), (0,)), ((), ())),
                preferred_element_type=jnp.float32,
            )
            total = term if total is None else total + term
        for h in range(2):
            value = total[h * count : (h + 1) * count] + total[(2 + h) * count : (3 + h) * count]
            at = h * half_width + c
            for other in others:
                value = value + other[:, at : at + step].astype(jnp.float32)
            out_ref[:, at : at + step] = value.astype(jnp.bfloat16)


def combine(exp_dev, dst, slot, gate, pieces, others=()):
    n = len(pieces)
    rows, half_width = pieces[0].shape
    count = slot.shape[1]
    return pl.pallas_call(
        functools.partial(combine_kernel, exp_dev, n),
        out_shape=jax.ShapeDtypeStruct((count, 2 * half_width), jnp.bfloat16),
        in_specs=[SMEM] + [VMEM] * (2 + n + len(others)),
        out_specs=VMEM,
        compiler_params=BIG,
        cost_estimate=pl.CostEstimate(
            flops=8 * n * rows * count * half_width,
            bytes_accessed=2 * n * rows * half_width + 4 * (1 + len(others)) * count * half_width,
            transcendentals=0,
        ),
        name="combine",
    )(dst, slot, gate, *pieces, *others)


def balance_kernel(n_group, size, mine_ref, own_ref, gt_ref, et_ref, *refs):
    blocks, (plan_ref, fac_ref) = refs[:-2], refs[-2:]
    sums = [[b[:, size + g, :] for g in range(n_group)] for b in blocks]
    targets = [gt_ref[g : g + 1, :] for g in range(n_group)]
    lanes = own_ref.shape[1]

    def inverse(parts, scale):
        return 1.0 / sum(part * s for part, s in zip(parts, scale))

    def first(step, carry):
        scale = carry[:n_group]
        rows = [inverse(s, scale) for s in sums]
        new = []
        for g in range(n_group):
            total = sum(s[g] * r for s, r in zip(sums, rows))
            total = jnp.sum(jnp.sum(total, 0, keepdims=True), 1, keepdims=True)
            new.append(targets[g] / jnp.broadcast_to(total, (1, lanes)))
        return tuple(new) + scale

    scales = tuple(jnp.ones((1, lanes), jnp.float32) for _ in range(2 * n_group))
    for step in range(ITER1):
        scales = first(step, scales)
    now, before = scales[:n_group], scales[n_group:]
    own = [own_ref[g : g + 1, :] for g in range(n_group)]
    own_rows = inverse(own, before)
    for g in range(n_group):
        plan_ref[g : g + 1, :] = own_rows * own[g] * now[g]
    mine = mine_ref[0]
    plans = []
    for s in sums:
        rows = inverse(s, before)
        chosen = sum(jnp.where(mine == g, s[g] * now[g], 0.0) for g in range(n_group))
        plans.append(rows * chosen)

    fac_ref[...] = jnp.ones_like(fac_ref)

    @pl.loop(0, ITER2)
    def _(step):
        fac = fac_ref[size:, :]
        total = jnp.zeros((size, lanes), jnp.float32)
        for b, plan in zip(blocks, plans):
            scores = b[:, :size, :]
            row = plan / jnp.sum(scores * fac[None], 1)
            total = total + jnp.sum(scores * row[:, None, :], 0)
        total = jnp.broadcast_to(jnp.sum(total, 1, keepdims=True), (size, lanes))
        fac_ref[:size, :] = fac
        fac_ref[size:, :] = et_ref[...] / total


def gating_kernel(size, factor, group_ref, scores_ref, plan_ref, dest_ref, *refs):
    facs, out_ref = refs[:-1], refs[-1]
    topk, count = dest_ref.shape
    total = [jnp.zeros((1, count), jnp.float32) for _ in range(topk)]
    index = lax.broadcasted_iota(jnp.int32, (size, count), 0)
    for k, fac in enumerate(facs):
        group = group_ref[k]
        scores = scores_ref[pl.ds(pl.multiple_of(group * size, 8), size), :]
        row = plan_ref[pl.ds(group, 1), :] / jnp.sum(scores * fac[:size, :], 0, keepdims=True)
        balanced = row * scores * fac[size:, :]
        expert = index + group * size
        for i in range(topk):
            hit = jnp.where(dest_ref[i : i + 1, :] == expert, balanced, 0.0)
            total[i] = total[i] + jnp.sum(hit, 0, keepdims=True)
    for i in range(topk):
        out_ref[i : i + 1, :] = total[i] * factor


def per_device(
    tokens, router_weight, expert_dest, group_capacity, expert_capacity, w_gate, w_up, w_down
):
    count, width = tokens.shape
    experts = router_weight.shape[1]
    topk = expert_dest.shape[1]
    n_group, n_plane, n_side = (lax.axis_size(a) for a in ALL)
    devices = n_group * n_plane * n_side
    exp_dev = w_gate.shape[0]
    size = experts // n_group
    n_peer = n_group * n_side
    group, plane, side = (lax.axis_index(a) for a in ALL)
    peer = group * n_side + side

    def cross(value, k, axis, n):
        return lax.ppermute(value, axis, [(i, i ^ k) for i in range(n)]) if k else value

    def shift(value, s):
        pairs = [(i, (i + s) % n_plane) for i in range(n_plane)]
        return lax.ppermute(value, "plane", pairs) if s % n_plane else value

    peers = [peer ^ k for k in range(n_peer)]
    dst = jnp.stack([((p // n_side) * n_plane + plane) * n_side + p % n_side for p in peers])
    dst = dst.astype(jnp.int32)

    named = expert_dest[:, :, None] == jnp.arange(experts, dtype=jnp.int32)[None, None, :]
    member = jnp.any(named, 1).astype(jnp.bfloat16)
    order = jnp.arange(count)
    earlier = (order[:, None] > order[None, :]).astype(jnp.bfloat16)
    before = jnp.dot(earlier, member, preferred_element_type=jnp.float32)
    rank = jnp.sum(jnp.where(named, before[:, None, :], 0.0), 2).astype(jnp.int32)
    dest_t = expert_dest.T
    slot_t = dest_t * SLOT_CAP + rank.T

    logits = jnp.dot(tokens, router_weight, preferred_element_type=jnp.float32)
    scores = jnp.exp(logits).T
    pad = round_up(n_group, 8)
    sums = jnp.pad(jnp.sum(scores.reshape(n_group, size, count), 1), ((0, pad - n_group), (0, 0)))
    held = []
    for k in range(n_group):
        part = lax.dynamic_slice_in_dim(scores, (group ^ k) * size, size, 0)
        held.append(cross(jnp.concatenate([part, sums], 0), k, "group", n_group))
    held = jnp.stack(held)
    held = jnp.concatenate([held] + [cross(held, k, "side", n_side) for k in range(1, n_side)], 0)

    shifts = [0] + sorted(range(1, n_plane), key=lambda s: (min(s, n_plane - s), s))
    toks = {s: shift(tokens, s) for s in shifts}
    slots = {s: shift(slot_t, s) for s in shifts}

    sent = {s: pack(exp_dev, dst, slots[s], toks[s]) for s in shifts}
    came = {
        s: [cross(sent[s][k], k, PLANE, n_peer) for k in range(n_peer)] for s in shifts
    }
    back = {}
    for i in range(0, n_plane, 2):
        pair = shifts[i : i + 2]
        made = ffn([p for s in pair for p in came[s]], w_gate, w_up, w_down)
        for j, s in enumerate(pair):
            mine = made[j * n_peer : (j + 1) * n_peer]
            back[s] = [cross(mine[k], k, PLANE, n_peer) for k in range(n_peer)]

    gcap = group_capacity.astype(jnp.float32)
    gtarget = count * devices * gcap / jnp.sum(gcap)
    ecap = expert_capacity.astype(jnp.float32).reshape(n_group, size)
    etarget = (gtarget / jnp.sum(ecap, 1))[:, None] * ecap
    own_target = lax.dynamic_index_in_dim(etarget, group, 0, keepdims=False)
    held = [shift(held, s) for s in shifts]
    plan, fac = pl.pallas_call(
        functools.partial(balance_kernel, n_group, size),
        out_shape=[
            jax.ShapeDtypeStruct((pad, count), jnp.float32),
            jax.ShapeDtypeStruct((2 * size, count), jnp.float32),
        ],
        in_specs=[SMEM] + [VMEM] * (3 + n_plane),
        out_specs=[VMEM] * 2,
        compiler_params=BIG,
        name="balance",
    )(
        group.astype(jnp.int32)[None],
        sums,
        jnp.broadcast_to(gtarget[:, None], (n_group, count)),
        jnp.broadcast_to(own_target[:, None], (size, count)),
        *held,
    )
    facs = [cross(fac, k, "group", n_group) for k in range(n_group)]
    gating_t = pl.pallas_call(
        functools.partial(gating_kernel, size, experts / topk),
        out_shape=jax.ShapeDtypeStruct((topk, count), jnp.float32),
        in_specs=[SMEM] + [VMEM] * (3 + n_group),
        out_specs=VMEM,
        compiler_params=BIG,
        name="gating",
    )(
        jnp.stack([group ^ k for k in range(n_group)]).astype(jnp.int32),
        scores,
        plan,
        dest_t,
        *facs,
    )
    gates = {s: shift(gating_t, s) for s in shifts}

    partials = [
        shift(combine(exp_dev, dst, slots[s], gates[s], back[s]), -s) for s in shifts if s
    ]
    mixed = combine(exp_dev, dst, slots[0], gates[0], back[0], partials)
    return mixed, gating_t.T


def solution(mesh):
    n_group, n_lane = mesh.shape["group"], mesh.shape["expert"]
    n_side = 2 if n_lane % 2 == 0 else 1
    fine = Mesh(mesh.devices.reshape(n_group, n_lane // n_side, n_side), ALL)
    rows = P(ALL, None)
    stack = P(ALL, None, None)
    return jax.shard_map(
        per_device,
        mesh=fine,
        in_specs=(rows, P(), rows, P(), P(), stack, stack, stack),
        out_specs=(rows, rows),
        check_vma=False,
    )
```

```python
import functools

import jax
import jax.numpy as jnp
from jax import lax
from jax.experimental import pallas as pl
from jax.experimental.pallas import tpu as pltpu
from jax.sharding import Mesh
from jax.sharding import PartitionSpec as P


ITER1 = 10
ITER2 = 10
SLOT_CAP = 9
MAIN = 8

ALL = ("group", "plane", "side")
PLANE = ("group", "side")
VMEM = pl.BlockSpec(memory_space=pltpu.VMEM)
SMEM = pl.BlockSpec(memory_space=pltpu.SMEM)
BIG = pltpu.CompilerParams(vmem_limit_bytes=60 << 20)


def round_up(value, step):
    return -(-value // step) * step


def piece_rows(exp_dev):
    return round_up(2 * exp_dev * SLOT_CAP, 8)


def row_slots(exp_dev, shape):
    row = lax.broadcasted_iota(jnp.int32, shape, 0)
    last = row - 2 * MAIN * exp_dev
    main = last < 0
    expert = jnp.where(main, lax.shift_right_logical(row, 4), lax.shift_right_logical(last, 1))
    half = jnp.where(main, lax.shift_right_logical(row, 3) & 1, last & 1)
    rank = jnp.where(main, row & 7, MAIN)
    slot = jnp.where(last >= 2 * exp_dev, -1, expert * SLOT_CAP + rank)
    return slot, half


def pack_kernel(exp_dev, dst_ref, slot_ref, tok_ref, *outs):
    rows, half_width = outs[0].shape
    topk, count = slot_ref.shape
    local, half = row_slots(exp_dev, (rows, count))
    low, high = [], []
    for k in range(len(outs)):
        want = jnp.where(local < 0, -1, local + dst_ref[k] * (exp_dev * SLOT_CAP))
        hit = jnp.zeros((rows, count), jnp.float32)
        for i in range(topk):
            hit = jnp.where(slot_ref[i : i + 1, :] == want, 1.0, hit)
        low.append(jnp.where(half == 0, hit, 0.0))
        high.append(jnp.where(half == 1, hit, 0.0))
    pick = jnp.concatenate(
        [jnp.concatenate(low, 0), jnp.concatenate(high, 0)], 1
    ).astype(jnp.bfloat16)
    step = min(512, half_width)
    for c in range(0, half_width, step):
        both = jnp.concatenate(
            [tok_ref[:, h * half_width + c : h * half_width + c + step] for h in range(2)], 0
        )
        got = jnp.dot(pick, both, preferred_element_type=jnp.float32)
        for k, out in enumerate(outs):
            out[:, c : c + step] = got[k * rows : (k + 1) * rows].astype(jnp.bfloat16)


def pack(exp_dev, dst, slot, tok):
    rows, width = piece_rows(exp_dev), tok.shape[1]
    n = dst.shape[0]
    return pl.pallas_call(
        functools.partial(pack_kernel, exp_dev),
        out_shape=[jax.ShapeDtypeStruct((rows, width // 2), jnp.bfloat16)] * n,
        in_specs=[SMEM, VMEM, VMEM],
        out_specs=[VMEM] * n,
        compiler_params=BIG,
        cost_estimate=pl.CostEstimate(
            flops=2 * n * rows * tok.shape[0] * width,
            bytes_accessed=2 * tok.size + n * rows * width,
            transcendentals=0,
        ),
        name="pack",
    )(dst, slot, tok)


def ffn_kernel(n, exp_dev, low, high, *refs):
    final = high == exp_dev
    refs = list(refs)

    def take(many):
        got = refs[:many]
        del refs[:many]
        return got

    mains, tails = take(n), take(n)
    weights = take(3)
    if low:
        (given_ref,) = take(1)
        take(n)
    outs = take(n)
    if not final:
        (rest_ref,) = take(1)
    x_ref, last_ref, res_ref, gate_ref, up_ref, down_ref, sems = refs
    buffers = (gate_ref, up_ref, down_ref)
    step_id = pl.program_id(0)
    half_width = mains[0].shape[1]
    step = min(1024, half_width)
    many = high - low

    def load(e, j):
        slot = lax.rem(e, 2)
        return pltpu.make_async_copy(weights[j].at[low + e], buffers[j].at[slot], sems.at[slot, j])

    @pl.when(step_id == 0)
    def _():
        for e in range(min(2, many)):
            for j in range(3):
                load(e, j).start()
        for c in range(0, half_width, step):
            tiles = [p[:8, c : c + step].astype(jnp.float32) for p in tails]
            last_ref[:, c : c + step] = jnp.concatenate(tiles, 0).astype(jnp.bfloat16)
        if low:
            res_ref[: low * n, :] = given_ref[...]

    @pl.when(step_id < many)
    def _():
        e = step_id
        for i in range(0, n, 2):
            for c in range(0, half_width, step):
                a = mains[i][:, c : c + step].astype(jnp.float32)
                b = mains[i + 1][:, c : c + step].astype(jnp.float32)
                for h in range(2):
                    both = jnp.concatenate([a[h * 8 : h * 8 + 8], b[h * 8 : h * 8 + 8]], 0)
                    x_ref[i * 8 : i * 8 + 16, h * half_width + c : h * half_width + c + step] = (
                        both.astype(jnp.bfloat16)
                    )
        row = lax.broadcasted_iota(jnp.int32, (n, 8 * n), 0)
        col = lax.broadcasted_iota(jnp.int32, (n, 8 * n), 1)
        for h in range(2):
            pick = jnp.where(col == row * 8 + (low + e) * 2 + h, 1.0, 0.0).astype(jnp.bfloat16)
            for c in range(0, half_width, step):
                x_ref[8 * n :, h * half_width + c : h * half_width + c + step] = jnp.dot(
                    pick, last_ref[:, c : c + step], preferred_element_type=jnp.float32
                ).astype(jnp.bfloat16)
        slot = lax.rem(e, 2)
        rest = pl.ds(pl.multiple_of((low + e) * n, n), n)
        load(e, 0).wait()
        gate = jnp.dot(x_ref[...], gate_ref[slot], preferred_element_type=jnp.float32)
        load(e, 1).wait()
        up = jnp.dot(x_ref[...], up_ref[slot], preferred_element_type=jnp.float32)
        hidden = (gate / (1.0 + jnp.exp(-gate)) * up).astype(jnp.bfloat16)
        load(e, 2).wait()
        for c in range(0, half_width, step):
            down = [
                jnp.dot(
                    hidden,
                    down_ref[slot, :, h * half_width + c : h * half_width + c + step],
                    preferred_element_type=jnp.float32,
                )
                for h in range(2)
            ]
            for i in range(n):
                both = jnp.concatenate([d[i * 8 : i * 8 + 8] for d in down], 0)
                outs[i][:, c : c + step] = both.astype(jnp.bfloat16)
            for h in range(2):
                res_ref[rest, h * half_width + c : h * half_width + c + step] = down[h][
                    8 * n :
                ].astype(jnp.bfloat16)

    @pl.when(step_id + 2 < many)
    def _():
        for j in range(3):
            load(step_id + 2, j).start()

    if not final:

        @pl.when(step_id == many - 1)
        def _():
            rest_ref[...] = res_ref[: high * n, :]

    else:

        @pl.when(step_id == many)
        def _():
            row = lax.broadcasted_iota(jnp.int32, (8 * n, exp_dev * n), 0)
            col = lax.broadcasted_iota(jnp.int32, (8 * n, exp_dev * n), 1)
            hit = col == lax.shift_right_logical(row & 7, 1) * n + lax.shift_right_logical(row, 3)
            for c in range(0, half_width, step):
                got = None
                for h in range(2):
                    pick = jnp.where(hit & ((row & 1) == h), 1.0, 0.0).astype(jnp.bfloat16)
                    term = jnp.dot(
                        pick,
                        res_ref[:, h * half_width + c : h * half_width + c + step],
                        preferred_element_type=jnp.float32,
                    )
                    got = term if got is None else got + term
                for i in range(n):
                    outs[i][:8, c : c + step] = got[i * 8 : i * 8 + 8].astype(jnp.bfloat16)


def ffn(pieces, w_gate, w_up, w_down, low, high, so_far=()):
    n = len(pieces)
    exp_dev, width, hidden = w_gate.shape
    rows, half_width = pieces[0].shape
    final = high == exp_dev
    tile = 2 * MAIN
    main = pl.BlockSpec((tile, half_width), lambda e: (jnp.minimum(low + e, exp_dev - 1), 0))
    tail = pl.BlockSpec((tile, half_width), lambda e: (exp_dev, 0), pipeline_mode=pl.Buffered(1))
    made = pl.BlockSpec((tile, half_width), lambda e: (low + e, 0))
    whole = pl.BlockSpec(memory_space=pl.ANY)
    total = SLOT_CAP * n
    in_specs = [main] * n + [tail] * n + [whole] * 3
    args = [*pieces, *pieces, w_gate, w_up, w_down]
    aliases = {}
    if low:
        before, given = so_far[:n], so_far[n]
        in_specs += [pl.BlockSpec((low * n, width), lambda e: (0, 0))] + [whole] * n
        aliases = {len(args) + 1 + i: i for i in range(n)}
        args += [given, *before]
    out_shape = [jax.ShapeDtypeStruct((rows, half_width), jnp.bfloat16)] * n
    out_specs = [made] * n
    if not final:
        out_shape.append(jax.ShapeDtypeStruct((high * n, width), jnp.bfloat16))
        out_specs.append(pl.BlockSpec((high * n, width), lambda e: (0, 0)))
    return pl.pallas_call(
        functools.partial(ffn_kernel, n, exp_dev, low, high),
        grid=(high - low + (1 if final else 0),),
        out_shape=out_shape,
        in_specs=in_specs,
        out_specs=out_specs,
        input_output_aliases=aliases,
        scratch_shapes=[
            pltpu.VMEM((total, width), jnp.bfloat16),
            pltpu.VMEM((8 * n, half_width), jnp.bfloat16),
            pltpu.VMEM((exp_dev * n, width), jnp.bfloat16),
            pltpu.VMEM((2, width, hidden), jnp.bfloat16),
            pltpu.VMEM((2, width, hidden), jnp.bfloat16),
            pltpu.VMEM((2, hidden, width), jnp.bfloat16),
            pltpu.SemaphoreType.DMA((2, 3)),
        ],
        compiler_params=pltpu.CompilerParams(
            dimension_semantics=("arbitrary",), vmem_limit_bytes=60 << 20
        ),
        cost_estimate=pl.CostEstimate(
            flops=6 * (high - low) * total * width * hidden,
            bytes_accessed=6 * (high - low) * width * hidden + 4 * n * rows * half_width,
            transcendentals=(high - low) * total * hidden,
        ),
        name="ffn",
    )(*args)


def combine_kernel(exp_dev, n, halves, joined, dst_ref, slot_ref, gate_ref, *refs):
    outs = refs[-1:] if joined else refs[-len(halves) :]
    pieces, others = refs[:n], refs[n : -len(outs)]
    rows, half_width = pieces[0].shape
    topk, count = slot_ref.shape
    local, half = row_slots(exp_dev, (rows, count))
    depth = round_up(n * rows, 128)
    fill = depth - n * rows
    weights = []
    for k in range(n):
        want = jnp.where(local < 0, -1, local + dst_ref[k] * (exp_dev * SLOT_CAP))
        weight = jnp.zeros((rows, count), jnp.float32)
        for i in range(topk):
            weight = jnp.where(slot_ref[i : i + 1, :] == want, gate_ref[i : i + 1, :], weight)
        weights.append(weight)
    coarse, rest = [], []
    for h in halves:
        parts = [jnp.where(half == h, weight, 0.0) for weight in weights]
        if fill:
            parts.append(jnp.zeros((fill, count), jnp.float32))
        turned = jnp.concatenate(parts, 0).T
        coarse.append(turned.astype(jnp.bfloat16))
        rest.append((turned - coarse[-1].astype(jnp.float32)).astype(jnp.bfloat16))
    weights = jnp.concatenate(coarse + rest, 0)
    step = min(512, half_width)
    for c in range(0, half_width, step):
        parts = [piece[:, c : c + step].astype(jnp.float32) for piece in pieces]
        if fill:
            parts.append(jnp.zeros((fill, step), jnp.float32))
        total = jnp.dot(
            weights,
            jnp.concatenate(parts, 0).astype(jnp.bfloat16),
            preferred_element_type=jnp.float32,
        )
        m = len(halves)
        for i, h in enumerate(halves):
            value = total[i * count : (i + 1) * count]
            value = value + total[(m + i) * count : (m + i + 1) * count]
            for other in others[i::m]:
                value = value + other[:, c : c + step].astype(jnp.float32)
            value = value.astype(jnp.bfloat16)
            if joined:
                outs[0][:, h * half_width + c : h * half_width + c + step] = value
            else:
                outs[i][:, c : c + step] = value


def combine(exp_dev, dst, slot, gate, pieces, others=(), halves=(0, 1), joined=False):
    n, m = len(pieces), len(halves)
    rows, half_width = pieces[0].shape
    count = slot.shape[1]
    wide = 2 * half_width if joined else half_width
    return pl.pallas_call(
        functools.partial(combine_kernel, exp_dev, n, halves, joined),
        out_shape=[jax.ShapeDtypeStruct((count, wide), jnp.bfloat16)] * (1 if joined else m),
        in_specs=[SMEM] + [VMEM] * (2 + n + len(others)),
        out_specs=[VMEM] * (1 if joined else m),
        compiler_params=BIG,
        cost_estimate=pl.CostEstimate(
            flops=4 * m * n * rows * count * half_width,
            bytes_accessed=2 * n * rows * half_width + 2 * (m + len(others)) * count * half_width,
            transcendentals=0,
        ),
        name="combine",
    )(dst, slot, gate, *pieces, *others)


def balance_kernel(n_group, size, mine_ref, own_ref, gt_ref, et_ref, *refs):
    blocks, (plan_ref, fac_ref) = refs[:-2], refs[-2:]
    sums = [[b[:, size + g, :] for g in range(n_group)] for b in blocks]
    targets = [gt_ref[g : g + 1, :] for g in range(n_group)]
    lanes = own_ref.shape[1]

    def inverse(parts, scale):
        return 1.0 / sum(part * s for part, s in zip(parts, scale))

    def first(carry):
        scale = carry[:n_group]
        rows = [inverse(s, scale) for s in sums]
        new = []
        for g in range(n_group):
            total = sum(s[g] * r for s, r in zip(sums, rows))
            total = jnp.sum(jnp.sum(total, 0, keepdims=True), 1, keepdims=True)
            new.append(targets[g] / jnp.broadcast_to(total, (1, lanes)))
        return tuple(new) + scale

    scales = tuple(jnp.ones((1, lanes), jnp.float32) for _ in range(2 * n_group))
    for _ in range(ITER1):
        scales = first(scales)
    now, before = scales[:n_group], scales[n_group:]
    own = [own_ref[g : g + 1, :] for g in range(n_group)]
    own_rows = inverse(own, before)
    for g in range(n_group):
        plan_ref[g : g + 1, :] = own_rows * own[g] * now[g]
    mine = mine_ref[0]
    plans = []
    for s in sums:
        rows = inverse(s, before)
        chosen = sum(jnp.where(mine == g, s[g] * now[g], 0.0) for g in range(n_group))
        plans.append(rows * chosen)

    fac_ref[...] = jnp.ones_like(fac_ref)

    @pl.loop(0, ITER2)
    def _(step):
        fac = fac_ref[size:, :]
        total = jnp.zeros((size, lanes), jnp.float32)
        for b, plan in zip(blocks, plans):
            scores = b[:, :size, :]
            row = plan / jnp.sum(scores * fac[None], 1)
            total = total + jnp.sum(scores * row[:, None, :], 0)
        total = jnp.broadcast_to(jnp.sum(total, 1, keepdims=True), (size, lanes))
        fac_ref[:size, :] = fac
        fac_ref[size:, :] = et_ref[...] / total


def gating_kernel(size, factor, group_ref, scores_ref, plan_ref, dest_ref, *refs):
    facs, out_ref = refs[:-1], refs[-1]
    topk, count = dest_ref.shape
    total = [jnp.zeros((1, count), jnp.float32) for _ in range(topk)]
    index = lax.broadcasted_iota(jnp.int32, (size, count), 0)
    for k, fac in enumerate(facs):
        group = group_ref[k]
        scores = scores_ref[pl.ds(pl.multiple_of(group * size, 8), size), :]
        row = plan_ref[pl.ds(group, 1), :] / jnp.sum(scores * fac[:size, :], 0, keepdims=True)
        balanced = row * scores * fac[size:, :]
        expert = index + group * size
        for i in range(topk):
            hit = jnp.where(dest_ref[i : i + 1, :] == expert, balanced, 0.0)
            total[i] = total[i] + jnp.sum(hit, 0, keepdims=True)
    for i in range(topk):
        out_ref[i : i + 1, :] = total[i] * factor


def per_device(
    tokens, router_weight, expert_dest, group_capacity, expert_capacity, w_gate, w_up, w_down
):
    count, _ = tokens.shape
    experts = router_weight.shape[1]
    topk = expert_dest.shape[1]
    n_group, n_plane, n_side = (lax.axis_size(a) for a in ALL)
    devices = n_group * n_plane * n_side
    exp_dev = w_gate.shape[0]
    size = experts // n_group
    n_peer = n_group * n_side
    group, plane, side = (lax.axis_index(a) for a in ALL)
    peer = group * n_side + side

    def cross(value, k, axis, n):
        return lax.ppermute(value, axis, [(i, i ^ k) for i in range(n)]) if k else value

    def shift(value, s):
        pairs = [(i, (i + s) % n_plane) for i in range(n_plane)]
        return lax.ppermute(value, "plane", pairs) if s % n_plane else value

    def after(value, *deps):
        return lax.optimization_barrier((value, *deps))[0]

    peers = [peer ^ k for k in range(n_peer)]
    dst = jnp.stack([((p // n_side) * n_plane + plane) * n_side + p % n_side for p in peers])
    dst = dst.astype(jnp.int32)

    half = n_plane // 2
    shifts = [0] + sorted(range(1, n_plane), key=lambda s: (min(s, n_plane - s), s))
    toks = {0: tokens}
    for s in shifts[1:]:
        step = 1 if s <= half else -1
        toks[s] = shift(toks[(s - step) % n_plane], step)

    named = expert_dest[:, :, None] == jnp.arange(experts, dtype=jnp.int32)[None, None, :]
    member = jnp.any(named, 1).astype(jnp.bfloat16)
    order = jnp.arange(count)
    earlier = (order[:, None] > order[None, :]).astype(jnp.bfloat16)
    before = jnp.dot(earlier, member, preferred_element_type=jnp.float32)
    rank = jnp.sum(jnp.where(named, before[:, None, :], 0.0), 2).astype(jnp.int32)
    dest_t = expert_dest.T
    slot_t = dest_t * SLOT_CAP + rank.T
    slots = {}
    for s in shifts:
        slots[s] = shift(slot_t, s)

    def send(pieces):
        out = []
        for k in range(n_peer):
            out.append(cross(pieces[k], k, PLANE, n_peer))
        return out

    def packed(s):
        return pack(exp_dev, dst, slots[s], toks[s])

    def feed(i):
        group_of = pairs[i]
        given = [p for s in group_of for p in came[s]]
        cut = exp_dev // 2 if i == 0 else 0
        so_far = ()
        if cut:
            so_far = ffn(given, w_gate, w_up, w_down, 0, cut)
        made = ffn(given, w_gate, w_up, w_down, cut, exp_dev, so_far)
        return {s: made[j * n_peer : (j + 1) * n_peer] for j, s in enumerate(group_of)}

    sent, came, made, back = {}, {}, {}, {}
    pairs = [shifts[i : i + 2] for i in range(0, n_plane, 2)]
    sent[0] = packed(0)
    came[0] = send(sent[0])

    logits = jnp.dot(
        tokens, after(router_weight, sent[0][0]), preferred_element_type=jnp.float32
    )
    scores = jnp.exp(logits).T
    pad = round_up(n_group, 8)
    sums = jnp.pad(jnp.sum(scores.reshape(n_group, size, count), 1), ((0, pad - n_group), (0, 0)))
    held = []
    for k in range(n_group):
        part = lax.dynamic_slice_in_dim(scores, (group ^ k) * size, size, 0)
        held.append(cross(jnp.concatenate([part, sums], 0), k, "group", n_group))

    last = None
    for s in pairs[0][1:]:
        sent[s] = packed(s)
        came[s] = send(sent[s])
        last = sent[s][0]
    if last is not None:
        held = [after(h, last) for h in held]
    held = jnp.stack(held)
    held = jnp.concatenate([held] + [cross(held, k, "side", n_side) for k in range(1, n_side)], 0)
    for s in shifts:
        if s not in sent and s in (pairs + [[]])[1]:
            sent[s] = packed(s)
            came[s] = send(sent[s])
    spread = []
    for s in shifts:
        spread.append(shift(held, s))
    made.update(feed(0))
    for s in shifts:
        if s not in sent:
            sent[s] = packed(s)
            came[s] = send(sent[s])

    gcap = group_capacity.astype(jnp.float32)
    gtarget = count * devices * gcap / jnp.sum(gcap)
    ecap = expert_capacity.astype(jnp.float32).reshape(n_group, size)
    etarget = (gtarget / jnp.sum(ecap, 1))[:, None] * ecap
    own_target = lax.dynamic_index_in_dim(etarget, group, 0, keepdims=False)
    plan, fac = pl.pallas_call(
        functools.partial(balance_kernel, n_group, size),
        out_shape=[
            jax.ShapeDtypeStruct((pad, count), jnp.float32),
            jax.ShapeDtypeStruct((2 * size, count), jnp.float32),
        ],
        in_specs=[SMEM] + [VMEM] * (3 + n_plane),
        out_specs=[VMEM] * 2,
        compiler_params=BIG,
        cost_estimate=pl.CostEstimate(
            flops=8 * ITER2 * experts * count * devices // n_group,
            bytes_accessed=4 * size * count * devices,
            transcendentals=0,
        ),
        name="balance",
    )(
        group.astype(jnp.int32)[None],
        after(sums, made[0][0]),
        jnp.broadcast_to(gtarget[:, None], (n_group, count)),
        jnp.broadcast_to(own_target[:, None], (size, count)),
        *spread,
    )
    facs = []
    for k in range(n_group):
        facs.append(cross(fac, k, "group", n_group))

    early = [s for s in pairs[0] if s]
    for s in early:
        back[s] = send([after(p, plan) for p in made[s]])
    for i in range(1, len(pairs)):
        made.update(feed(i))
    late = [s for group_of in pairs[1:] for s in group_of][::-1]
    for s in late:
        back[s] = send(made[s])

    gating_t = pl.pallas_call(
        functools.partial(gating_kernel, size, experts / topk),
        out_shape=jax.ShapeDtypeStruct((topk, count), jnp.float32),
        in_specs=[SMEM] + [VMEM] * (3 + n_group),
        out_specs=VMEM,
        compiler_params=BIG,
        name="gating",
    )(
        jnp.stack([group ^ k for k in range(n_group)]).astype(jnp.int32),
        scores,
        after(plan, made[late[-1]][0]) if late else plan,
        dest_t,
        *facs,
    )
    gates = {}
    for s in shifts:
        gates[s] = shift(gating_t, s)

    def combined(s, others, halves, joined=False):
        return combine(
            exp_dev, dst, slots[s], gates[s], back[s], others, halves=halves, joined=joined
        )

    back[0] = send(made[0])
    near = (n_plane - 1) // 2
    gone = []
    for chain, step in ((range(near, 0, -1), -1), (range(near + 1, n_plane), 1)):
        running = ()
        for s in chain:
            if running:
                value = [combined(s, running[h : h + 1], (h,))[0] for h in range(2)]
            else:
                value = combined(s, (), (0, 1))
            running = []
            for h in range(2):
                running.append(shift(value[h], step))
        gone += running
    mixed = combined(0, gone, (0, 1), joined=True)[0]
    return mixed, gating_t.T


def solution(mesh):
    n_group, n_lane = mesh.shape["group"], mesh.shape["expert"]
    n_side = 2 if n_lane % 2 == 0 else 1
    fine = Mesh(mesh.devices.reshape(n_group, n_lane // n_side, n_side), ALL)
    rows = P(ALL, None)
    stack = P(ALL, None, None)

    return jax.shard_map(
        per_device,
        mesh=fine,
        in_specs=(rows, P(), rows, P(), P(), stack, stack, stack),
        out_specs=(rows, rows),
        check_vma=False,
    )
```

```python
import functools

import jax
import jax.numpy as jnp
from jax import lax
from jax.experimental import pallas as pl
from jax.experimental.pallas import tpu as pltpu
from jax.sharding import Mesh
from jax.sharding import PartitionSpec as P


ITER1 = 10
ITER2 = 10
SLOT_CAP = 9
MAIN = 8

ALL = ("group", "plane", "side")
PLANE = ("group", "side")
VMEM = pl.BlockSpec(memory_space=pltpu.VMEM)
SMEM = pl.BlockSpec(memory_space=pltpu.SMEM)
BIG = pltpu.CompilerParams(vmem_limit_bytes=60 << 20)


def round_up(value, step):
    return -(-value // step) * step


def piece_rows(exp_dev):
    return round_up(2 * exp_dev * SLOT_CAP, 8)


def row_slots(exp_dev, shape):
    row = lax.broadcasted_iota(jnp.int32, shape, 0)
    last = row - 2 * MAIN * exp_dev
    main = last < 0
    expert = jnp.where(main, lax.shift_right_logical(row, 4), lax.shift_right_logical(last, 1))
    half = jnp.where(main, lax.shift_right_logical(row, 3) & 1, last & 1)
    rank = jnp.where(main, row & 7, MAIN)
    slot = jnp.where(last >= 2 * exp_dev, -1, expert * SLOT_CAP + rank)
    return slot, half


def pack_kernel(exp_dev, dst_ref, slot_ref, tok_ref, *outs):
    rows, half_width = outs[0].shape
    topk, count = slot_ref.shape
    local, half = row_slots(exp_dev, (rows, count))
    low, high = [], []
    for k in range(len(outs)):
        want = jnp.where(local < 0, -1, local + dst_ref[k] * (exp_dev * SLOT_CAP))
        hit = jnp.zeros((rows, count), jnp.float32)
        for i in range(topk):
            hit = jnp.where(slot_ref[i : i + 1, :] == want, 1.0, hit)
        low.append(jnp.where(half == 0, hit, 0.0))
        high.append(jnp.where(half == 1, hit, 0.0))
    pick = jnp.concatenate(
        [jnp.concatenate(low, 0), jnp.concatenate(high, 0)], 1
    ).astype(jnp.bfloat16)
    step = min(512, half_width)
    for c in range(0, half_width, step):
        both = jnp.concatenate(
            [tok_ref[:, h * half_width + c : h * half_width + c + step] for h in range(2)], 0
        )
        got = jnp.dot(pick, both, preferred_element_type=jnp.float32)
        for k, out in enumerate(outs):
            out[:, c : c + step] = got[k * rows : (k + 1) * rows].astype(jnp.bfloat16)


def pack(exp_dev, dst, slot, tok):
    rows, width = piece_rows(exp_dev), tok.shape[1]
    n = dst.shape[0]
    return pl.pallas_call(
        functools.partial(pack_kernel, exp_dev),
        out_shape=[jax.ShapeDtypeStruct((rows, width // 2), jnp.bfloat16)] * n,
        in_specs=[SMEM, VMEM, VMEM],
        out_specs=[VMEM] * n,
        compiler_params=BIG,
        cost_estimate=pl.CostEstimate(
            flops=2 * n * rows * tok.shape[0] * width,
            bytes_accessed=2 * tok.size + n * rows * width,
            transcendentals=0,
        ),
        name="pack",
    )(dst, slot, tok)


def ffn_kernel(n, exp_dev, low, high, *refs):
    final = high == exp_dev
    refs = list(refs)

    def take(many):
        got = refs[:many]
        del refs[:many]
        return got

    mains, tails = take(n), take(n)
    weights = take(3)
    if low:
        (given_ref,) = take(1)
        take(n)
    outs = take(n)
    if not final:
        (rest_ref,) = take(1)
    x_ref, last_ref, res_ref, gate_ref, up_ref, down_ref, sems = refs
    buffers = (gate_ref, up_ref, down_ref)
    step_id = pl.program_id(0)
    half_width = mains[0].shape[1]
    step = min(1024, half_width)
    many = high - low

    def load(e, j):
        slot = lax.rem(e, 2)
        return pltpu.make_async_copy(weights[j].at[low + e], buffers[j].at[slot], sems.at[slot, j])

    @pl.when(step_id == 0)
    def _():
        for e in range(min(2, many)):
            for j in range(3):
                load(e, j).start()
        for c in range(0, half_width, step):
            tiles = [p[:8, c : c + step].astype(jnp.float32) for p in tails]
            last_ref[:, c : c + step] = jnp.concatenate(tiles, 0).astype(jnp.bfloat16)
        if low:
            res_ref[: low * n, :] = given_ref[...]

    @pl.when(step_id < many)
    def _():
        e = step_id
        for i in range(0, n, 2):
            for c in range(0, half_width, step):
                a = mains[i][:, c : c + step].astype(jnp.float32)
                b = mains[i + 1][:, c : c + step].astype(jnp.float32)
                for h in range(2):
                    both = jnp.concatenate([a[h * 8 : h * 8 + 8], b[h * 8 : h * 8 + 8]], 0)
                    x_ref[i * 8 : i * 8 + 16, h * half_width + c : h * half_width + c + step] = (
                        both.astype(jnp.bfloat16)
                    )
        row = lax.broadcasted_iota(jnp.int32, (n, 8 * n), 0)
        col = lax.broadcasted_iota(jnp.int32, (n, 8 * n), 1)
        for h in range(2):
            pick = jnp.where(col == row * 8 + (low + e) * 2 + h, 1.0, 0.0).astype(jnp.bfloat16)
            for c in range(0, half_width, step):
                x_ref[8 * n :, h * half_width + c : h * half_width + c + step] = jnp.dot(
                    pick, last_ref[:, c : c + step], preferred_element_type=jnp.float32
                ).astype(jnp.bfloat16)
        slot = lax.rem(e, 2)
        rest = pl.ds(pl.multiple_of((low + e) * n, n), n)
        load(e, 0).wait()
        gate = jnp.dot(x_ref[...], gate_ref[slot], preferred_element_type=jnp.float32)
        load(e, 1).wait()
        up = jnp.dot(x_ref[...], up_ref[slot], preferred_element_type=jnp.float32)
        hidden = (gate / (1.0 + jnp.exp(-gate)) * up).astype(jnp.bfloat16)
        load(e, 2).wait()
        for c in range(0, half_width, step):
            down = [
                jnp.dot(
                    hidden,
                    down_ref[slot, :, h * half_width + c : h * half_width + c + step],
                    preferred_element_type=jnp.float32,
                )
                for h in range(2)
            ]
            for i in range(n):
                both = jnp.concatenate([d[i * 8 : i * 8 + 8] for d in down], 0)
                outs[i][:, c : c + step] = both.astype(jnp.bfloat16)
            for h in range(2):
                res_ref[rest, h * half_width + c : h * half_width + c + step] = down[h][
                    8 * n :
                ].astype(jnp.bfloat16)

    @pl.when(step_id + 2 < many)
    def _():
        for j in range(3):
            load(step_id + 2, j).start()

    if not final:

        @pl.when(step_id == many - 1)
        def _():
            rest_ref[...] = res_ref[: high * n, :]

    else:

        @pl.when(step_id == many)
        def _():
            row = lax.broadcasted_iota(jnp.int32, (8 * n, exp_dev * n), 0)
            col = lax.broadcasted_iota(jnp.int32, (8 * n, exp_dev * n), 1)
            hit = col == lax.shift_right_logical(row & 7, 1) * n + lax.shift_right_logical(row, 3)
            for c in range(0, half_width, step):
                got = None
                for h in range(2):
                    pick = jnp.where(hit & ((row & 1) == h), 1.0, 0.0).astype(jnp.bfloat16)
                    term = jnp.dot(
                        pick,
                        res_ref[:, h * half_width + c : h * half_width + c + step],
                        preferred_element_type=jnp.float32,
                    )
                    got = term if got is None else got + term
                for i in range(n):
                    outs[i][:8, c : c + step] = got[i * 8 : i * 8 + 8].astype(jnp.bfloat16)


def ffn(pieces, w_gate, w_up, w_down, low, high, so_far=()):
    n = len(pieces)
    exp_dev, width, hidden = w_gate.shape
    rows, half_width = pieces[0].shape
    final = high == exp_dev
    tile = 2 * MAIN
    main = pl.BlockSpec((tile, half_width), lambda e: (jnp.minimum(low + e, exp_dev - 1), 0))
    tail = pl.BlockSpec((tile, half_width), lambda e: (exp_dev, 0), pipeline_mode=pl.Buffered(1))
    made = pl.BlockSpec((tile, half_width), lambda e: (low + e, 0))
    whole = pl.BlockSpec(memory_space=pl.ANY)
    total = SLOT_CAP * n
    in_specs = [main] * n + [tail] * n + [whole] * 3
    args = [*pieces, *pieces, w_gate, w_up, w_down]
    aliases = {}
    if low:
        before, given = so_far[:n], so_far[n]
        in_specs += [pl.BlockSpec((low * n, width), lambda e: (0, 0))] + [whole] * n
        aliases = {len(args) + 1 + i: i for i in range(n)}
        args += [given, *before]
    out_shape = [jax.ShapeDtypeStruct((rows, half_width), jnp.bfloat16)] * n
    out_specs = [made] * n
    if not final:
        out_shape.append(jax.ShapeDtypeStruct((high * n, width), jnp.bfloat16))
        out_specs.append(pl.BlockSpec((high * n, width), lambda e: (0, 0)))
    return pl.pallas_call(
        functools.partial(ffn_kernel, n, exp_dev, low, high),
        grid=(high - low + (1 if final else 0),),
        out_shape=out_shape,
        in_specs=in_specs,
        out_specs=out_specs,
        input_output_aliases=aliases,
        scratch_shapes=[
            pltpu.VMEM((total, width), jnp.bfloat16),
            pltpu.VMEM((8 * n, half_width), jnp.bfloat16),
            pltpu.VMEM((exp_dev * n, width), jnp.bfloat16),
            pltpu.VMEM((2, width, hidden), jnp.bfloat16),
            pltpu.VMEM((2, width, hidden), jnp.bfloat16),
            pltpu.VMEM((2, hidden, width), jnp.bfloat16),
            pltpu.SemaphoreType.DMA((2, 3)),
        ],
        compiler_params=pltpu.CompilerParams(
            dimension_semantics=("arbitrary",), vmem_limit_bytes=60 << 20
        ),
        cost_estimate=pl.CostEstimate(
            flops=6 * (high - low) * total * width * hidden,
            bytes_accessed=6 * (high - low) * width * hidden + 4 * n * rows * half_width,
            transcendentals=(high - low) * total * hidden,
        ),
        name="ffn",
    )(*args)


def combine_kernel(exp_dev, n, halves, joined, dst_ref, slot_ref, gate_ref, *refs):
    outs = refs[-1:] if joined else refs[-len(halves) :]
    pieces, others = refs[:n], refs[n : -len(outs)]
    rows, half_width = pieces[0].shape
    topk, count = slot_ref.shape
    local, half = row_slots(exp_dev, (rows, count))
    depth = round_up(n * rows, 128)
    fill = depth - n * rows
    weights = []
    for k in range(n):
        want = jnp.where(local < 0, -1, local + dst_ref[k] * (exp_dev * SLOT_CAP))
        weight = jnp.zeros((rows, count), jnp.float32)
        for i in range(topk):
            weight = jnp.where(slot_ref[i : i + 1, :] == want, gate_ref[i : i + 1, :], weight)
        weights.append(weight)
    coarse, rest = [], []
    for h in halves:
        parts = [jnp.where(half == h, weight, 0.0) for weight in weights]
        if fill:
            parts.append(jnp.zeros((fill, count), jnp.float32))
        turned = jnp.concatenate(parts, 0).T
        coarse.append(turned.astype(jnp.bfloat16))
        rest.append((turned - coarse[-1].astype(jnp.float32)).astype(jnp.bfloat16))
    weights = jnp.concatenate(coarse + rest, 0)
    step = min(512, half_width)
    for c in range(0, half_width, step):
        parts = [piece[:, c : c + step].astype(jnp.float32) for piece in pieces]
        if fill:
            parts.append(jnp.zeros((fill, step), jnp.float32))
        total = jnp.dot(
            weights,
            jnp.concatenate(parts, 0).astype(jnp.bfloat16),
            preferred_element_type=jnp.float32,
        )
        m = len(halves)
        for i, h in enumerate(halves):
            value = total[i * count : (i + 1) * count]
            value = value + total[(m + i) * count : (m + i + 1) * count]
            for other in others[i::m]:
                value = value + other[:, c : c + step].astype(jnp.float32)
            value = value.astype(jnp.bfloat16)
            if joined:
                outs[0][:, h * half_width + c : h * half_width + c + step] = value
            else:
                outs[i][:, c : c + step] = value


def combine(exp_dev, dst, slot, gate, pieces, others=(), halves=(0, 1), joined=False):
    n, m = len(pieces), len(halves)
    rows, half_width = pieces[0].shape
    count = slot.shape[1]
    wide = 2 * half_width if joined else half_width
    return pl.pallas_call(
        functools.partial(combine_kernel, exp_dev, n, halves, joined),
        out_shape=[jax.ShapeDtypeStruct((count, wide), jnp.bfloat16)] * (1 if joined else m),
        in_specs=[SMEM] + [VMEM] * (2 + n + len(others)),
        out_specs=[VMEM] * (1 if joined else m),
        compiler_params=BIG,
        cost_estimate=pl.CostEstimate(
            flops=4 * m * n * rows * count * half_width,
            bytes_accessed=2 * n * rows * half_width + 2 * (m + len(others)) * count * half_width,
            transcendentals=0,
        ),
        name="combine",
    )(dst, slot, gate, *pieces, *others)


def balance_kernel(n_group, size, mine_ref, own_ref, gt_ref, et_ref, *refs):
    blocks, (plan_ref, fac_ref) = refs[:-2], refs[-2:]
    sums = [[b[:, size + g, :] for g in range(n_group)] for b in blocks]
    targets = [gt_ref[g : g + 1, :] for g in range(n_group)]
    lanes = own_ref.shape[1]

    def inverse(parts, scale):
        return 1.0 / sum(part * s for part, s in zip(parts, scale))

    def first(carry):
        scale = carry[:n_group]
        rows = [inverse(s, scale) for s in sums]
        new = []
        for g in range(n_group):
            total = sum(s[g] * r for s, r in zip(sums, rows))
            total = jnp.sum(jnp.sum(total, 0, keepdims=True), 1, keepdims=True)
            new.append(targets[g] / jnp.broadcast_to(total, (1, lanes)))
        return tuple(new) + scale

    scales = tuple(jnp.ones((1, lanes), jnp.float32) for _ in range(2 * n_group))
    for _ in range(ITER1):
        scales = first(scales)
    now, before = scales[:n_group], scales[n_group:]
    own = [own_ref[g : g + 1, :] for g in range(n_group)]
    own_rows = inverse(own, before)
    for g in range(n_group):
        plan_ref[g : g + 1, :] = own_rows * own[g] * now[g]
    mine = mine_ref[0]
    plans = []
    for s in sums:
        rows = inverse(s, before)
        chosen = sum(jnp.where(mine == g, s[g] * now[g], 0.0) for g in range(n_group))
        plans.append(rows * chosen)

    fac_ref[...] = jnp.ones_like(fac_ref)

    @pl.loop(0, ITER2)
    def _(step):
        fac = fac_ref[size:, :]
        total = jnp.zeros((size, lanes), jnp.float32)
        for b, plan in zip(blocks, plans):
            scores = b[:, :size, :]
            row = plan / jnp.sum(scores * fac[None], 1)
            total = total + jnp.sum(scores * row[:, None, :], 0)
        total = jnp.broadcast_to(jnp.sum(total, 1, keepdims=True), (size, lanes))
        fac_ref[:size, :] = fac
        fac_ref[size:, :] = et_ref[...] / total


def gating_kernel(size, factor, group_ref, scores_ref, plan_ref, dest_ref, *refs):
    facs, out_ref = refs[:-1], refs[-1]
    topk, count = dest_ref.shape
    total = [jnp.zeros((1, count), jnp.float32) for _ in range(topk)]
    index = lax.broadcasted_iota(jnp.int32, (size, count), 0)
    for k, fac in enumerate(facs):
        group = group_ref[k]
        scores = scores_ref[pl.ds(pl.multiple_of(group * size, 8), size), :]
        row = plan_ref[pl.ds(group, 1), :] / jnp.sum(scores * fac[:size, :], 0, keepdims=True)
        balanced = row * scores * fac[size:, :]
        expert = index + group * size
        for i in range(topk):
            hit = jnp.where(dest_ref[i : i + 1, :] == expert, balanced, 0.0)
            total[i] = total[i] + jnp.sum(hit, 0, keepdims=True)
    for i in range(topk):
        out_ref[i : i + 1, :] = total[i] * factor


def per_device(
    tokens, router_weight, expert_dest, group_capacity, expert_capacity, w_gate, w_up, w_down
):
    count, _ = tokens.shape
    experts = router_weight.shape[1]
    topk = expert_dest.shape[1]
    n_group, n_plane, n_side = (lax.axis_size(a) for a in ALL)
    devices = n_group * n_plane * n_side
    exp_dev = w_gate.shape[0]
    size = experts // n_group
    n_peer = n_group * n_side
    group, plane, side = (lax.axis_index(a) for a in ALL)
    peer = group * n_side + side

    def cross(value, k, axis, n):
        return lax.ppermute(value, axis, [(i, i ^ k) for i in range(n)]) if k else value

    def shift(value, s):
        pairs = [(i, (i + s) % n_plane) for i in range(n_plane)]
        return lax.ppermute(value, "plane", pairs) if s % n_plane else value

    peers = [peer ^ k for k in range(n_peer)]
    dst = jnp.stack([((p // n_side) * n_plane + plane) * n_side + p % n_side for p in peers])
    dst = dst.astype(jnp.int32)

    half = n_plane // 2
    shifts = [0] + sorted(range(1, n_plane), key=lambda s: (min(s, n_plane - s), s))
    toks = {0: tokens}
    for s in shifts[1:]:
        step = 1 if s <= half else -1
        toks[s] = shift(toks[(s - step) % n_plane], step)

    named = expert_dest[:, :, None] == jnp.arange(experts, dtype=jnp.int32)[None, None, :]
    member = jnp.any(named, 1).astype(jnp.bfloat16)
    order = jnp.arange(count)
    earlier = (order[:, None] > order[None, :]).astype(jnp.bfloat16)
    before = jnp.dot(earlier, member, preferred_element_type=jnp.float32)
    rank = jnp.sum(jnp.where(named, before[:, None, :], 0.0), 2).astype(jnp.int32)
    dest_t = expert_dest.T
    slot_t = dest_t * SLOT_CAP + rank.T
    slots = {}
    for s in shifts:
        slots[s] = shift(slot_t, s)

    def send(pieces):
        out = {}
        for k in reversed(range(n_peer)):
            out[k] = cross(pieces[k], k, PLANE, n_peer)
        return [out[k] for k in range(n_peer)]

    def packed(s):
        return pack(exp_dev, dst, slots[s], toks[s])

    def feed(i):
        group_of = pairs[i]
        given = [p for s in group_of for p in came[s]]
        cut = exp_dev // 2 if i == 0 else 0
        so_far = ()
        if cut:
            so_far = ffn(given, w_gate, w_up, w_down, 0, cut)
        made = ffn(given, w_gate, w_up, w_down, cut, exp_dev, so_far)
        return {s: made[j * n_peer : (j + 1) * n_peer] for j, s in enumerate(group_of)}

    sent, came, made, back = {}, {}, {}, {}
    pairs = [shifts[i : i + 2] for i in range(0, n_plane, 2)]
    sent[0] = packed(0)
    came[0] = send(sent[0])

    logits = jnp.dot(tokens, router_weight, preferred_element_type=jnp.float32)
    scores = jnp.exp(logits).T
    pad = round_up(n_group, 8)
    sums = jnp.pad(jnp.sum(scores.reshape(n_group, size, count), 1), ((0, pad - n_group), (0, 0)))
    held = []
    for k in range(n_group):
        part = lax.dynamic_slice_in_dim(scores, (group ^ k) * size, size, 0)
        held.append(cross(jnp.concatenate([part, sums], 0), k, "group", n_group))

    for s in pairs[0][1:]:
        sent[s] = packed(s)
        came[s] = send(sent[s])
    held = jnp.stack(held)
    held = jnp.concatenate([held] + [cross(held, k, "side", n_side) for k in range(1, n_side)], 0)
    gcap = group_capacity.astype(jnp.float32)
    gtarget = count * devices * gcap / jnp.sum(gcap)
    ecap = expert_capacity.astype(jnp.float32).reshape(n_group, size)
    etarget = (gtarget / jnp.sum(ecap, 1))[:, None] * ecap
    own_target = lax.dynamic_index_in_dim(etarget, group, 0, keepdims=False)
    held, gtarget, own_target = lax.optimization_barrier(
        (
            held,
            jnp.broadcast_to(gtarget[:, None], (n_group, count)),
            jnp.broadcast_to(own_target[:, None], (size, count)),
        )
    )
    for s in shifts:
        if s not in sent and s in (pairs + [[]])[1]:
            sent[s] = packed(s)
            came[s] = send(sent[s])
    spread = []
    for s in shifts:
        spread.append(shift(held, s))
    made.update(feed(0))
    for s in shifts:
        if s not in sent:
            sent[s] = packed(s)
            came[s] = send(sent[s])

    plan, fac = pl.pallas_call(
        functools.partial(balance_kernel, n_group, size),
        out_shape=[
            jax.ShapeDtypeStruct((pad, count), jnp.float32),
            jax.ShapeDtypeStruct((2 * size, count), jnp.float32),
        ],
        in_specs=[SMEM] + [VMEM] * (3 + n_plane),
        out_specs=[VMEM] * 2,
        compiler_params=BIG,
        cost_estimate=pl.CostEstimate(
            flops=8 * ITER2 * experts * count * devices // n_group,
            bytes_accessed=4 * size * count * devices,
            transcendentals=0,
        ),
        name="balance",
    )(
        group.astype(jnp.int32)[None],
        sums,
        gtarget,
        own_target,
        *spread,
    )
    facs = []
    for k in range(n_group):
        facs.append(cross(fac, k, "group", n_group))

    early = [s for s in pairs[0] if s]
    for s in early:
        back[s] = send(made[s])
    for i in range(1, len(pairs)):
        made.update(feed(i))
    late = [s for group_of in pairs[1:] for s in group_of][::-1]
    for s in late:
        back[s] = send(made[s])

    gating_t = pl.pallas_call(
        functools.partial(gating_kernel, size, experts / topk),
        out_shape=jax.ShapeDtypeStruct((topk, count), jnp.float32),
        in_specs=[SMEM] + [VMEM] * (3 + n_group),
        out_specs=VMEM,
        compiler_params=BIG,
        name="gating",
    )(
        jnp.stack([group ^ k for k in range(n_group)]).astype(jnp.int32),
        scores,
        plan,
        dest_t,
        *facs,
    )
    gates = {}
    for s in shifts:
        gates[s] = shift(gating_t, s)

    def combined(s, others, halves, joined=False):
        return combine(
            exp_dev, dst, slots[s], gates[s], back[s], others, halves=halves, joined=joined
        )

    back[0] = send(made[0])
    near = (n_plane - 1) // 2
    gone = []
    for chain, step in ((range(near, 0, -1), -1), (range(near + 1, n_plane), 1)):
        running = ()
        for s in chain:
            if running:
                value = [combined(s, running[h : h + 1], (h,))[0] for h in range(2)]
            else:
                value = combined(s, (), (0, 1))
            running = []
            for h in range(2):
                running.append(shift(value[h], step))
        gone += running
    mixed = combined(0, gone, (0, 1), joined=True)[0]
    return mixed, gating_t.T


def solution(mesh):
    n_group, n_lane = mesh.shape["group"], mesh.shape["expert"]
    n_side = 2 if n_lane % 2 == 0 else 1
    fine = Mesh(mesh.devices.reshape(n_group, n_lane // n_side, n_side), ALL)
    rows = P(ALL, None)
    stack = P(ALL, None, None)

    return jax.shard_map(
        per_device,
        mesh=fine,
        in_specs=(rows, P(), rows, P(), P(), stack, stack, stack),
        out_specs=(rows, rows),
        check_vma=False,
    )
```
